32 devices in a mesh: gx: 4 (over z), gy: 4 (over x, core), gz: 2 (over y).
Axes of the slice: x: 2, y: 2, z: 4, core: 2. Of those that a mesh axis runs over, the one named last changes fastest.
Arguments:
- response: float32 [32, 32, 12, 128], P('gx', 'gy', 'gz'), may hold values from -3 to 3
- source: float32 [32, 32, 12, 128], P('gx', 'gy', 'gz'), may hold values from -6 to 6
- occupied: float32 [32, 32, 12, 2048], P('gx', 'gy', 'gz'), may hold values from -0.0546875 to 0.0546875
- potential: float32 [32, 32, 12], P('gx', 'gy', 'gz'), may hold values from 0 to 2
- energy_shift: float32 [128], replicated, may hold values from 0.5 to 2
Outputs:
- updated: float32 [32, 32, 12, 128], P('gx', 'gy', 'gz')
- projected: float32 [32, 32, 12, 128], P('gx', 'gy', 'gz')
The draws below stay inside these ranges and needn't reach their ends.
All inputs are finite; a program needn't handle non-finite values.
Results may differ from the reference program's by a relative error of at most 0.00011.
Values sent between devices are 32-bit elements; how exact they have to be, the bound alone decides.
No kernel may reach another device: no remote copies, remote signals or barrier semaphores. Data moves between devices by JAX's collectives and lax.ppermute only.
A program may use at most 64 MiB of HBM per device.

```python
import math
import jax
import jax.numpy as jnp
from jax import lax

OCC = 2048
RESP = 128
ITERS = 1
NX = 32
NY = 32
NZ = 12


def block_levels(key, shape, shards, least, high):
    gain, own = 1.0, jax.random.fold_in(key, 6)
    for position, blocks in shards:
        steps = jnp.exp(jax.random.uniform(jax.random.fold_in(own, position), (blocks,), jnp.float32, least / len(shards), high / len(shards)))
        gain = gain * jnp.repeat(steps, shape[position] // blocks).reshape([-1 if axis == position else 1 for axis in range(len(shape))])
    return gain


def gaussian(rng, dims, scale, reach, pieces=(), kind=jnp.bfloat16):
    loudness = block_levels(rng, dims, pieces, -0.22, 0.18) if pieces else 1.0
    entries = jax.random.normal(rng, dims, jnp.float32) * scale * loudness
    return jnp.minimum(jnp.maximum(entries, -reach), reach).astype(kind)


def setup_inputs(seed: int = 0) -> dict:
    streams_of = jax.random.split(jax.random.key(seed), 6)
    response = gaussian(streams_of[0], (NX, NY, NZ, RESP), 0.5, 3.0, ((0, 4), (1, 4), (2, 2)), jnp.float32)
    source = gaussian(streams_of[1], (NX, NY, NZ, RESP), 1.0, 6.0, ((0, 4), (1, 4), (2, 2)), jnp.float32)
    occupied = gaussian(streams_of[2], (NX, NY, NZ, OCC), (NX * NY * NZ) ** -0.5, 0.0546875, ((0, 4), (1, 4), (2, 2)), jnp.float32)
    potential = jnp.clip(2.0 * jax.random.uniform(streams_of[3], (NX, NY, NZ), jnp.float32) ** block_levels(streams_of[3], (NX, NY, NZ), ((0, 4), (1, 4), (2, 2)), -0.2, 0.2), 0.0, 2.0)
    energy_shift = jnp.clip(jnp.exp(jax.random.uniform(streams_of[4], (RESP,), jnp.float32, math.log(0.5), math.log(2.0))), 0.5, 2.0)
    return dict(response=response, source=source, occupied=occupied, potential=potential, energy_shift=energy_shift)


stencil_weights = (-5369.0 / 1800.0, 12.0 / 7.0, -15.0 / 56.0, 10.0 / 189.0, -1.0 / 112.0, 2.0 / 1925.0, -1.0 / 16632.0)
damping = 0.1
margin = 6


def laplacian(padded, span_first, span_second, span_third):
    centre = padded[margin:margin + span_first, margin:margin + span_second, margin:margin + span_third]
    summed = (3.0 * stencil_weights[0]) * centre
    for offset in range(1, margin + 1):
        beside = padded[margin + offset:margin + offset + span_first, margin:margin + span_second, margin:margin + span_third]
        beside = beside + padded[margin - offset:margin - offset + span_first, margin:margin + span_second, margin:margin + span_third]
        beside = beside + padded[margin:margin + span_first, margin + offset:margin + offset + span_second, margin:margin + span_third]
        beside = beside + padded[margin:margin + span_first, margin - offset:margin - offset + span_second, margin:margin + span_third]
        beside = beside + padded[margin:margin + span_first, margin:margin + span_second, margin + offset:margin + offset + span_third]
        beside = beside + padded[margin:margin + span_first, margin:margin + span_second, margin - offset:margin - offset + span_third]
        summed = summed + stencil_weights[offset] * beside
    return centre, summed


def residual_of(padded, potential, energy_shift, source):
    span_first, span_second, span_third = potential.shape
    centre, summed = laplacian(padded, span_first, span_second, span_third)
    return -0.5 * summed + (potential[:, :, :, None] + energy_shift) * centre + source


def reference(response, source, occupied, potential, energy_shift):
    span_first, span_second, span_third, orbitals = response.shape
    cell_count = span_first * span_second * span_third
    flat_occ = occupied.reshape(cell_count, occupied.shape[3])
    updated = response
    projected = response
    for iteration in range(ITERS):
        padded = jnp.pad(updated, ((margin, margin), (margin, margin), (margin, margin), (0, 0)))
        residual = residual_of(padded, potential, energy_shift, source)
        flat_res = residual.reshape(cell_count, orbitals)
        intersection = lax.dot_general(flat_occ, flat_res, (((0,), (0,)), ((), ())), precision=lax.Precision.HIGHEST, preferred_element_type=jnp.float32)
        removed = jnp.dot(flat_occ, intersection, precision=lax.Precision.HIGHEST, preferred_element_type=jnp.float32)
        projected = (flat_res - removed).reshape(updated.shape)
        updated = updated - damping * projected
    return updated, projected
```

```python
import functools

import jax
import jax.numpy as jnp
from jax import lax
from jax.experimental import pallas as pl
from jax.experimental.pallas import tpu as pltpu
from jax.sharding import PartitionSpec as P

stencil_weights = (
    -5369.0 / 1800.0,
    12.0 / 7.0,
    -15.0 / 56.0,
    10.0 / 189.0,
    -1.0 / 112.0,
    2.0 / 1925.0,
    -1.0 / 16632.0,
)
damping = 0.1
margin = 6
lanes = 128
axes = ("gx", "gy", "gz")


def is_power(count):
    return count & (count - 1) == 0


def plan(sizes, blocks):
    count_x, count_y, count_z = (sizes[name] for name in axes)
    places = [(x, y, z) for x in range(count_x) for y in range(count_y) for z in range(count_z)]
    index = {place: i for i, place in enumerate(places)}

    def bits(dim, low, count):
        return [(dim, 1 << k) for k in range(low, count.bit_length() - 1)]

    def route(place):
        core = place[1] & 1
        along_y, along_z = bits(1, 1, count_y), bits(2, 0, count_z)
        along_x = bits(0, 0, count_x) if is_power(count_x) else []
        return [(1, 1)] + (along_z + along_y if core else along_y + along_z) + along_x

    routes = [route(place) for place in places]
    halvings = min(blocks.bit_length() - 1, len(routes[0]))
    stages, kept = [], [0] * len(places)
    for stage in range(len(routes[0])):
        pairs = []
        for i, place in enumerate(places):
            dim, bit = routes[i][stage]
            other = list(place)
            other[dim] ^= bit
            pairs.append((i, index[tuple(other)]))
            if stage < halvings and place[dim] & bit:
                kept[i] |= 1 << (halvings - 1 - stage)
        stages.append(pairs)
    return stages, halvings, [(kept[a], kept[b]) for a, b in stages[0]]


def faces(block, axis, dim, span):
    count = lax.axis_size(axis)
    low_face = lax.slice_in_dim(block, 0, margin, axis=dim)
    high_face = lax.slice_in_dim(block, span - margin, span, axis=dim)
    if count == 2:
        position = lax.axis_index(axis)
        sent = low_face if span == margin else jnp.where(position == 0, high_face, low_face)
        beside = lax.ppermute(sent, axis, [(0, 1), (1, 0)])
        return jnp.where(position == 1, beside, 0.0), jnp.where(position == 0, beside, 0.0)
    forward = [(i, i + 1) for i in range(count - 1)]
    below = lax.ppermute(high_face, axis, forward)
    above = lax.ppermute(low_face, axis, [(b, a) for a, b in forward])
    return below, above


def sum_beside(padded, dim, span, offset):
    return lax.slice_in_dim(
        padded, margin + offset, margin + offset + span, axis=dim
    ) + lax.slice_in_dim(padded, margin - offset, margin - offset + span, axis=dim)


def residual_of(block, padded, potential, energy_shift, source):
    summed = 3.0 * stencil_weights[0] * block
    for offset in range(1, margin + 1):
        beside = sum_beside(padded[0], 0, block.shape[0], offset)
        beside = beside + sum_beside(padded[1], 1, block.shape[1], offset)
        beside = beside + sum_beside(padded[2], 2, block.shape[2], offset)
        summed = summed + stencil_weights[offset] * beside
    return -0.5 * summed + (potential[:, :, :, None] + energy_shift) * block + source


def product(a, b, dims):
    return lax.dot_general(
        a, b, (dims, ((), ())), precision=lax.Precision.HIGHEST, preferred_element_type=jnp.float32
    )


def intersect_kernel(order_ref, res_ref, occ_ref, kept_ref, sent_ref):
    res = res_ref[...]
    for side, target in enumerate((kept_ref, sent_ref)):
        order = order_ref[side]
        swap = order & 1
        for at in range(0, target.shape[0], 2):
            first = at ^ (order & -2)
            columns = pl.ds(pl.multiple_of(first * lanes, 2 * lanes), 2 * lanes)
            both = product(res, occ_ref[:, columns], ((0,), (0,)))
            target[at + swap] = both[:, :lanes]
            target[at + 1 - swap] = both[:, lanes:]


def remove_kernel(order_ref, res_ref, old_ref, occ_ref, kept_ref, came_ref, new_ref, out_ref):
    total = res_ref[...]
    for side, origin in enumerate((kept_ref, came_ref)):
        order = order_ref[side]
        swap = order & 1
        for at in range(0, origin.shape[0], 2):
            first = at ^ (order & -2)
            columns = pl.ds(pl.multiple_of(first * lanes, 2 * lanes), 2 * lanes)
            both = jnp.concatenate([origin[at + swap], origin[at + 1 - swap]], axis=1)
            total = total - product(occ_ref[:, columns], both, ((1,), (1,)))
    out_ref[...] = total
    new_ref[...] = old_ref[...] - damping * total


def shards(sizes, response, source, occupied, potential, energy_shift):
    block, source = response.transpose(0, 2, 1, 3), source.transpose(0, 2, 1, 3)
    potential = potential.transpose(0, 2, 1)
    span_x, span_z, span_y, orbitals = block.shape
    cells = span_x * span_y * span_z
    count = occupied.shape[3]
    flat_occ = occupied.transpose(0, 2, 1, 3).reshape(cells, count)
    blocks = count // lanes
    stages, halvings, kept_of = plan(sizes, blocks)
    position = lax.axis_index(axes)
    order = jnp.array(kept_of, jnp.int32)[position]

    beside_z = faces(block, "gz", 1, span_z)
    beside_x = faces(block, "gx", 0, span_x)
    beside_y = faces(block, "gy", 2, span_y)
    padded = [
        jnp.concatenate([below, block, above], axis=dim)
        for dim, (below, above) in enumerate((beside_x, beside_z, beside_y))
    ]
    residual = residual_of(block, padded, potential, energy_shift, source)
    flat_res = residual.reshape(cells, orbitals)

    scalar = pl.BlockSpec(memory_space=pltpu.SMEM)
    vector = pl.BlockSpec(memory_space=pltpu.VMEM)
    half = jax.ShapeDtypeStruct((blocks // 2, orbitals, lanes), jnp.float32)
    kept, sent = pl.pallas_call(
        intersect_kernel,
        out_shape=(half, half),
        in_specs=[scalar, vector, vector],
        out_specs=(vector, vector),
    )(order, flat_res, flat_occ)

    swapped = []
    for stage, pairs in enumerate(stages):
        if stage < halvings:
            came = lax.ppermute(sent, axes, pairs)
            if stage + 1 < halvings:
                middle = kept.shape[0] // 2
                sent = kept[middle:] + came[middle:]
                kept = kept[:middle] + came[:middle]
            else:
                kept = kept + came
        else:
            kept = kept + lax.ppermute(kept, axes, pairs)
    if not is_power(sizes["gx"]):
        kept = lax.psum(kept, "gx")
    for stage in reversed(range(halvings)):
        came = lax.ppermute(kept, axes, stages[stage])
        if stage:
            kept = jnp.concatenate([kept, came], axis=0)

    flat = jax.ShapeDtypeStruct((cells, orbitals), jnp.float32)
    updated, projected = pl.pallas_call(
        remove_kernel,
        out_shape=(flat, flat),
        in_specs=[scalar] + [vector] * 5,
        out_specs=(vector, vector),
    )(order, flat_res, block.reshape(cells, orbitals), flat_occ, kept, came)

    def back(array):
        return array.reshape(block.shape).transpose(0, 2, 1, 3)

    return back(updated), back(projected)


def solution(mesh):
    spec = P("gx", "gy", "gz", None)
    return jax.shard_map(
        functools.partial(shards, dict(mesh.shape)),
        mesh=mesh,
        in_specs=(spec, spec, spec, P("gx", "gy", "gz"), P()),
        out_specs=(spec, spec),
        check_vma=False,
    )
```

```python
import functools

import jax
import jax.numpy as jnp
from jax import lax
from jax.experimental import pallas as pl
from jax.experimental.pallas import tpu as pltpu
from jax.sharding import PartitionSpec as P

stencil_weights = (
    -5369.0 / 1800.0,
    12.0 / 7.0,
    -15.0 / 56.0,
    10.0 / 189.0,
    -1.0 / 112.0,
    2.0 / 1925.0,
    -1.0 / 16632.0,
)
damping = 0.1
margin = 6
lanes = 128
chunks = 2
mebibyte = 1 << 20
axes = ("gx", "gy", "gz")


def is_power(count):
    return count & (count - 1) == 0


def plan(sizes, blocks):
    count_x, count_y, count_z = (sizes[name] for name in axes)
    places = [(x, y, z) for x in range(count_x) for y in range(count_y) for z in range(count_z)]
    index = {place: i for i, place in enumerate(places)}

    def bits(dim, low, count):
        return [(dim, 1 << k) for k in range(low, count.bit_length() - 1)]

    def route(place):
        core = place[1] & 1
        along_y, along_z = bits(1, 1, count_y), bits(2, 0, count_z)
        along_x = bits(0, 0, count_x) if is_power(count_x) else []
        if core:
            return [(1, 1)] + along_z + along_y + along_x[::-1]
        return [(1, 1)] + along_y + along_z + along_x

    routes = [route(place) for place in places]
    flat = len(bits(1, 0, count_y)) + len(bits(2, 0, count_z))
    halvings = min(blocks.bit_length() - 1, flat)
    stages, kept = [], [0] * len(places)
    for stage in range(len(routes[0])):
        pairs = []
        for i, place in enumerate(places):
            dim, bit = routes[i][stage]
            other = list(place)
            other[dim] ^= bit
            pairs.append((i, index[tuple(other)]))
            if stage < halvings and place[dim] & bit:
                kept[i] |= 1 << (halvings - 1 - stage)
        stages.append(pairs)
    return stages, halvings, [(kept[a], kept[b]) for a, b in stages[0]]


def swaps(block, axis):
    count = lax.axis_size(axis)
    found = []
    for start in (0, 1):
        pairs = [(i, i + 1) for i in range(start, count - 1, 2)]
        if pairs:
            found.append(lax.ppermute(block, axis, pairs + [(b, a) for a, b in pairs]))
    return found


def product(a, b, dims):
    return lax.dot_general(
        a, b, (dims, ((), ())), precision=lax.Precision.HIGHEST, preferred_element_type=jnp.float32
    )


def weight(offset):
    return stencil_weights[offset] if offset <= margin else 0.0


def both_sides(refs, odd, shape):
    mine = refs[0]

    def at(index):
        first = mine[index]
        second = refs[1][index] if len(refs) > 1 else jnp.zeros_like(first)
        return jnp.where(odd, first, second), jnp.where(odd, second, first)

    return at


def stencil(odd_ref, block_ref, base_ref, beside_x, beside_z, beside_y, ext_ref, res_ref):
    span_x, span_z, span_y, orbitals = block_ref.shape
    odd_x, odd_y, odd_z = (odd_ref[i] != 0 for i in range(3))
    at_x = both_sides(beside_x, odd_x, None)
    at_y = both_sides(beside_y, odd_y, None)
    at_z = both_sides(beside_z, odd_z, None)
    for layer in range(margin):
        ext_ref[layer] = at_x(span_x - margin + layer)[0]
        ext_ref[margin + span_x + layer] = at_x(layer)[1]
    ext_ref[margin : margin + span_x] = block_ref[...]
    row = lax.broadcasted_iota(jnp.int32, (span_z, span_y, orbitals), 1)
    for x in range(span_x):
        block = block_ref[x]
        low_z, high_z = at_z(x)
        column = jnp.concatenate([low_z[span_z - margin :], block, high_z[:margin]], axis=0)
        summed = 3.0 * stencil_weights[0] * block
        for offset in range(1, margin + 1):
            beside = ext_ref[margin + x + offset] + ext_ref[margin + x - offset]
            beside = beside + column[margin + offset : margin + offset + span_z]
            beside = beside + column[margin - offset : margin - offset + span_z]
            summed = summed + stencil_weights[offset] * beside
        low_y, high_y = at_y(x)
        for turn in range(1, span_y):
            near = row < span_y - turn
            ahead, behind = weight(turn), weight(span_y - turn)
            inside = pltpu.roll(block, span_y - turn, 1)
            outside = pltpu.roll(jnp.where(row < turn, high_y, low_y), span_y - turn, 1)
            summed = summed + jnp.where(near, ahead, behind) * inside
            summed = summed + jnp.where(near, behind, ahead) * outside
        for offset in range(span_y, margin + 1):
            summed = summed + weight(offset) * (low_y + high_y)
        res_ref[pl.ds(x * span_z * span_y, span_z * span_y), :] = (
            base_ref[x] - 0.5 * summed
        ).reshape(span_z * span_y, orbitals)


def intersect(order_ref, res, occ_ref, start, kept_ref, sent_ref):
    for side, target in enumerate((sent_ref, kept_ref)):
        order = order_ref[1 - side]
        swap = order & 1
        for at in range(0, target.shape[0], 2):
            first = start + (at ^ (order & -2))
            columns = pl.ds(pl.multiple_of(first * lanes, 2 * lanes), 2 * lanes)
            both = product(res, occ_ref[:, columns], ((0,), (0,)))
            target[at + swap] = both[:, :lanes]
            target[at + 1 - swap] = both[:, lanes:]


def first_kernel(counts, order_ref, odd_ref, block_ref, base_ref, occ_ref, *refs):
    beside, at = [], 0
    for count in counts:
        beside.append(refs[at : at + count])
        at += count
    res_ref, kept_ref, sent_ref, ext_ref = refs[at:]
    stencil(odd_ref, block_ref, base_ref, *beside, ext_ref, res_ref)
    intersect(order_ref, res_ref[...], occ_ref, 0, kept_ref, sent_ref)


def later_kernel(start, order_ref, res_ref, occ_ref, kept_ref, sent_ref):
    intersect(order_ref, res_ref[...], occ_ref, start, kept_ref, sent_ref)


def remove(order_ref, total, occ_ref, start, kept_ref, came_ref):
    for side, origin in enumerate((kept_ref, came_ref)):
        order = order_ref[side]
        swap = order & 1
        for at in range(0, origin.shape[0], 2):
            first = start + (at ^ (order & -2))
            columns = pl.ds(pl.multiple_of(first * lanes, 2 * lanes), 2 * lanes)
            both = jnp.concatenate([origin[at + swap], origin[at + 1 - swap]], axis=1)
            total = total - product(occ_ref[:, columns], both, ((1,), (1,)))
    return total


def remove_kernel(start, order_ref, res_ref, occ_ref, kept_ref, came_ref, out_ref):
    out_ref[...] = remove(order_ref, res_ref[...], occ_ref, start, kept_ref, came_ref)


def last_kernel(start, order_ref, res_ref, occ_ref, kept_ref, came_ref, old_ref, new_ref, out_ref):
    total = remove(order_ref, res_ref[...], occ_ref, start, kept_ref, came_ref)
    out_ref[...] = total
    new_ref[...] = old_ref[...] - damping * total


scalar = pl.BlockSpec(memory_space=pltpu.SMEM)
vector = pl.BlockSpec(memory_space=pltpu.VMEM)


def call(kernel, outs, scalars, arrays, scratch=(), flops=0, name=None):
    shapes = [jax.ShapeDtypeStruct(shape, jnp.float32) for shape in outs]
    size = sum(4 * array.size for array in arrays) + sum(4 * shape.size for shape in shapes)
    return pl.pallas_call(
        kernel,
        out_shape=shapes,
        in_specs=[scalar] * len(scalars) + [vector] * len(arrays),
        out_specs=[vector] * len(shapes),
        scratch_shapes=list(scratch),
        cost_estimate=pl.CostEstimate(flops=flops, bytes_accessed=size, transcendentals=0),
        compiler_params=pltpu.CompilerParams(vmem_limit_bytes=16 * mebibyte),
        name=name,
    )(*scalars, *arrays)


def shards(sizes, response, source, occupied, potential, energy_shift):
    block, source = response.transpose(0, 2, 1, 3), source.transpose(0, 2, 1, 3)
    potential = potential.transpose(0, 2, 1)
    span_x, span_z, span_y, orbitals = block.shape
    cells = span_x * span_y * span_z
    count = occupied.shape[3]
    flat_occ = occupied.transpose(0, 2, 1, 3).reshape(cells, count)
    blocks = count // lanes // chunks
    stages, halvings, numbers = plan(sizes, blocks)
    place = [lax.axis_index(name) for name in axes]
    linear = (place[0] * sizes["gy"] + place[1]) * sizes["gz"] + place[2]
    order = jnp.array(numbers, jnp.int32)[linear]
    odd = jnp.stack(place) & 1

    beside_z = swaps(block, "gz")
    beside_x = swaps(block, "gx")
    beside_y = swaps(block, "gy")[::-1]
    beside_y = beside_y[::-1]
    base = (potential[:, :, :, None] + energy_shift) * block + source

    half = (blocks // 2, orbitals, lanes)
    work = 2 * cells * count * orbitals // chunks
    beside = (beside_x, beside_z, beside_y)
    flat_res, kept, sent = call(
        functools.partial(first_kernel, [len(found) for found in beside]),
        [(cells, orbitals), half, half],
        [order, odd],
        [block, base, flat_occ, *beside_x, *beside_z, *beside_y],
        [pltpu.VMEM((span_x + 2 * margin, span_z, span_y, orbitals), jnp.float32)],
        work,
        "first",
    )
    parts = [(kept, sent)]
    for chunk in range(1, chunks):
        parts.append(
            call(
                functools.partial(later_kernel, chunk * blocks),
                [half, half],
                [order],
                [flat_res, flat_occ],
                flops=work,
                name="later",
            )
        )
    for stage, pairs in enumerate(stages):
        for chunk, (kept, sent) in enumerate(parts):
            if stage < halvings:
                came = lax.ppermute(sent, axes, pairs)
                if stage + 1 < halvings:
                    middle = kept.shape[0] // 2
                    sent = kept[middle:] + came[middle:]
                    kept = kept[:middle] + came[:middle]
                else:
                    kept = kept + came
            else:
                kept = kept + lax.ppermute(kept, axes, pairs)
            parts[chunk] = (kept, sent)
    if not is_power(sizes["gx"]):
        parts = [(lax.psum(kept, "gx"), sent) for kept, sent in parts]
    for stage in reversed(range(halvings)):
        for chunk, (kept, came) in enumerate(parts):
            came = lax.ppermute(kept, axes, stages[stage])
            if stage:
                kept = jnp.concatenate([kept, came], axis=0)
            parts[chunk] = (kept, came)

    total = flat_res
    for chunk, (kept, came) in enumerate(parts[:-1]):
        (total,) = call(
            functools.partial(remove_kernel, chunk * blocks),
            [(cells, orbitals)],
            [order],
            [total, flat_occ, kept, came],
            flops=work,
            name="remove",
        )
    updated, projected = call(
        functools.partial(last_kernel, (chunks - 1) * blocks),
        [(cells, orbitals)] * 2,
        [order],
        [total, flat_occ, *parts[-1], block.reshape(cells, orbitals)],
        flops=work,
        name="last",
    )

    def back(array):
        return array.reshape(block.shape).transpose(0, 2, 1, 3)

    return back(updated), back(projected)


def solution(mesh):
    spec = P("gx", "gy", "gz", None)
    return jax.shard_map(
        functools.partial(shards, dict(mesh.shape)),
        mesh=mesh,
        in_specs=(spec, spec, spec, P("gx", "gy", "gz"), P()),
        out_specs=(spec, spec),
        check_vma=False,
    )
```
